32 devices in a mesh: dp: 8 (over y, x, core), filter: 4 (over z).
Axes of the slice: x: 2, y: 2, z: 4, core: 2. Of those that a mesh axis runs over, the one named last changes fastest.
Arguments:
- inputs: bfloat16 [8, 48, 24, 1024], P('dp', None, None, 'filter'), may hold values from -6 to 6
- kernel: bfloat16 [3, 3, 1024, 1024], P(None, None, 'filter'), may hold values from -0.0625 to 0.0625
- cotangent: bfloat16 [8, 48, 24, 1024], P('dp', 'filter'), may hold values from -6 to 6
Outputs:
- outputs: bfloat16 [8, 48, 24, 1024], P('dp', 'filter')
- input_grad: bfloat16 [8, 48, 24, 1024], P('dp', None, None, 'filter')
- kernel_grad: float32 [1024, 3, 3, 1024], P('dp', None, None, 'filter')
The draws below stay inside these ranges and needn't reach their ends.
All inputs are finite; a program needn't handle non-finite values.
Results may differ from the reference program's by a relative error of at most 0.001.
Values may be sent and summed in bfloat16 or wider, within the bound.
A program may use at most 128 MiB of HBM per device.

```python
import jax
import jax.numpy as jnp
from jax import lax

C = 1024
H = 48
W = 24
BATCH = 8


def strengthened(drawn, key, source, target, parts, factor):
    owner, partner = [(jnp.arange(drawn.shape[dim]) // (drawn.shape[dim] // parts)).reshape([-1 if axis == dim else 1 for axis in range(drawn.ndim)]) for dim in (source, target)]
    chosen = jax.random.permutation(key, parts)[partner]
    strong = (owner == chosen) | (owner == (partner + parts // 2) % parts)
    return jnp.where(strong, factor * drawn, drawn)


def level_of(rng, shape, split, least, top_value):
    gain, own = 1.0, jax.random.fold_in(rng, 6)
    for position, blocks in split:
        steps = jnp.exp(jax.random.uniform(jax.random.fold_in(own, position), (blocks,), jnp.float32, least / len(split), top_value / len(split)))
        gain = gain * jnp.repeat(steps, shape[position] // blocks).reshape([-1 if axis == position else 1 for axis in range(len(shape))])
    return gain


def bell_draw(rng, dims, spread, reach, cuts=(), kind=jnp.bfloat16):
    array = spread * jax.random.normal(rng, dims, jnp.float32)
    if cuts:
        array = array * level_of(rng, dims, cuts, -0.22, 0.18)
    return jnp.clip(array, -reach, reach).astype(kind)


def heavy_noise(own_key, extent, deviation, bound, pieces, heavy, held_as=jnp.bfloat16):
    values = deviation * jax.random.normal(own_key, extent, jnp.float32)
    if pieces:
        values = values * level_of(own_key, extent, pieces, -0.22, 0.18)
    return jnp.clip(strengthened(values, jax.random.fold_in(own_key, 3), *heavy), -bound, bound).astype(held_as)


def setup_inputs(seed: int = 0) -> dict:
    streams_of = jax.random.split(jax.random.key(seed), 4)
    return {
        "inputs": heavy_noise(streams_of[0], (BATCH, H, W, C), 1.0, 6.0, ((0, 8), (3, 4)), (3, 1, 4, 2.0)),
        "kernel": bell_draw(streams_of[1], (3, 3, C, C), (9 * C) ** -0.5, 0.0625, ((2, 4),)),
        "cotangent": heavy_noise(streams_of[2], (BATCH, H, W, C), 1.0, 6.0, ((0, 8), (1, 4)), (0, 3, 8, 2.0)),
    }


def one_sample(carry, pair):
    sample, grad_out = pair
    kernel_f = carry[1]
    xpad = jnp.pad(sample.astype(jnp.float32), ((1, 1), (1, 1), (0, 0)))
    gpad = jnp.pad(grad_out.astype(jnp.float32), ((1, 1), (1, 1), (0, 0)))
    result = jnp.zeros((H, W, C), jnp.float32)
    back = jnp.zeros((H, W, C), jnp.float32)
    taps = []
    for a in range(3):
        for b in range(3):
            result = result + jnp.einsum('hwi,io->hwo', xpad[a:a + H, b:b + W], kernel_f[a, b])
            back = back + jnp.einsum('hwo,io->hwi', gpad[2 - a:2 - a + H, 2 - b:2 - b + W], kernel_f[a, b])
            taps.append(jnp.einsum('hwi,hwo->oi', xpad[a:a + H, b:b + W], grad_out.astype(jnp.float32)))
    grads = jnp.stack(taps, 1).reshape(C, 3, 3, C)
    return ((carry[0] + grads, kernel_f), (result.astype(jnp.bfloat16), back.astype(jnp.bfloat16)))

def reference(inputs, kernel, cotangent):
    kernel_f = kernel.astype(jnp.float32)
    start = (jnp.zeros((C, 3, 3, C), jnp.float32), kernel_f)
    final, (outputs, input_grad) = lax.scan(one_sample, start, (inputs, cotangent))
    scale = 1.0 / jnp.sqrt(jnp.float32(BATCH * H * W))
    return (outputs, input_grad, final[0] * scale)
```

```python
import jax
import jax.numpy as jnp
from jax import lax
from jax.sharding import PartitionSpec as P


def gather_rows(block, groups, position):
    up, down = block, block
    above, below = [], []
    for step in range(1, groups):
        up = lax.ppermute(up, "filter", [(i, i + 1) for i in range(step - 1, groups - 1)])
        down = lax.ppermute(down, "filter", [(i, i - 1) for i in range(1, groups - step + 1)])
        below.insert(0, up)
        above.append(down)
    rows = block.shape[0]
    line = jnp.concatenate(below + [block] + above, 0)
    return lax.dynamic_slice_in_dim(line, (groups - 1 - position) * rows, groups * rows, 0)


def scatter_rows(partial, groups, position):
    cache = {}

    def at(offset):
        offset = offset % groups
        if offset not in cache:
            cache[offset] = partial(lax.rem(position + groups - offset, groups))
        return cache[offset]

    up, down = 0.0, 0.0
    for step in range(1, groups):
        up = lax.ppermute(at(step) + up, "filter", [(i, i + 1) for i in range(step)])
        down = lax.ppermute(
            at(groups - step) + down, "filter", [(i, i - 1) for i in range(groups - step, groups)]
        )
    return at(0) + up + down


def swap(value, bit, size):
    return lax.ppermute(value, "dp", [(i, i ^ (1 << bit)) for i in range(size)])


def pick(value, axis, index):
    return lax.dynamic_index_in_dim(value, index, axis, keepdims=False)


def on_device(inputs, kernel, cotangent):
    sample = inputs[0]
    height, width, local_in = sample.shape
    channels = kernel.shape[3]
    groups = lax.axis_size("filter")
    samples = lax.axis_size("dp")
    position = lax.axis_index("filter")
    place = lax.axis_index("dp")
    bits = samples.bit_length() - 1
    mine = [(place >> bit) & 1 for bit in range(bits)]
    my_rows = height // groups
    pad = ((1, 1), (1, 1), (0, 0))

    other = swap(sample, 0, samples)
    grad_rows = gather_rows(cotangent[0], groups, position)

    xpad = jnp.pad(sample, pad)

    def partial(block):
        rows = lax.dynamic_slice_in_dim(xpad, block * my_rows, my_rows + 2, 0)
        return lax.conv_general_dilated(
            rows[None], kernel, (1, 1), "VALID",
            dimension_numbers=("NHWC", "HWIO", "NHWC"),
            preferred_element_type=jnp.float32,
        )[0]

    outputs = scatter_rows(partial, groups, position).astype(jnp.bfloat16)[None]

    split = grad_rows.reshape(height, width, samples // 2, 2, channels // samples)
    own_half = pick(split, 3, mine[0])
    other_half = swap(pick(split, 3, 1 - mine[0]), 0, samples)
    pair_x = jnp.stack([xpad, jnp.pad(other, pad)])
    pair_g = jnp.stack([own_half, other_half])
    part = channels // samples // 2
    rest = list(range(1, bits))

    def weight_grad(cols):
        taps = [
            jnp.einsum(
                "nhwi,nhwo->oi",
                pair_x[:, a : a + height, b : b + width],
                cols,
                preferred_element_type=jnp.float32,
            )
            for a in range(3)
            for b in range(3)
        ]
        return jnp.stack(taps)

    plans = [rest, rest[::-1]]

    def columns(number, which):
        order = plans[number]
        cols = pair_g[..., number * part : (number + 1) * part]
        cols = cols.reshape((2, height, width) + (2,) * len(rest) + (part,))
        axis = 3 + (bits - 1 - order[0])
        index = mine[order[0]]
        chosen = pick(cols, axis, index if which else 1 - index)
        return chosen.reshape(2, height, width, -1)

    sent = weight_grad(jnp.concatenate([columns(0, False), columns(1, False)], -1))
    kept = weight_grad(jnp.concatenate([columns(0, True), columns(1, True)], -1))
    half = sent.shape[1] // 2
    finals = []
    for number, order in enumerate(plans):
        send = sent[:, number * half : (number + 1) * half]
        keep = kept[:, number * half : (number + 1) * half]
        left = sorted(order, reverse=True)
        for stage, bit in enumerate(order):
            total = keep + swap(send, bit, samples)
            left.remove(bit)
            if stage + 1 < len(order):
                total = total.reshape((9,) + (2,) * len(left) + (part, local_in))
                following = order[stage + 1]
                axis = 1 + left.index(following)
                send = pick(total, axis, 1 - mine[following]).reshape(9, -1, local_in)
                keep = pick(total, axis, mine[following]).reshape(9, -1, local_in)
        finals.append(total)
    scale = 1.0 / jnp.sqrt(jnp.float32(samples * height * width))
    grads = jnp.concatenate(finals, 1) * scale
    kernel_grad = grads.transpose(1, 0, 2).reshape(-1, 3, 3, local_in)

    input_grad = lax.conv_general_dilated(
        grad_rows[None], kernel[::-1, ::-1], (1, 1), "SAME",
        dimension_numbers=("NHWC", "HWOI", "NHWC"),
        preferred_element_type=jnp.float32,
    ).astype(jnp.bfloat16)
    return (outputs, input_grad, kernel_grad)


def solution(mesh):
    return jax.shard_map(
        on_device,
        mesh=mesh,
        in_specs=(
            P("dp", None, None, "filter"),
            P(None, None, "filter", None),
            P("dp", "filter", None, None),
        ),
        out_specs=(
            P("dp", "filter", None, None),
            P("dp", None, None, "filter"),
            P("dp", None, None, "filter"),
        ),
        check_vma=False,
    )
```

```python
import functools

import jax
import jax.numpy as jnp
from jax import lax
from jax.experimental import pallas as pl
from jax.experimental.pallas import tpu as pltpu
from jax.sharding import PartitionSpec as P


def gather_rows(block, groups, position):
    up, down = block, block
    above, below = [], []
    for step in range(1, groups):
        up = lax.ppermute(up, "filter", [(i, i + 1) for i in range(step - 1, groups - 1)])
        down = lax.ppermute(down, "filter", [(i, i - 1) for i in range(1, groups - step + 1)])
        below.insert(0, up)
        above.append(down)
    rows = block.shape[0]
    line = jnp.concatenate(below + [block] + above, 0)
    return lax.dynamic_slice_in_dim(line, (groups - 1 - position) * rows, groups * rows, 0)


def scatter_rows(partial, groups, position):
    cache = {}

    def at(offset):
        offset = offset % groups
        if offset not in cache:
            cache[offset] = partial(lax.rem(position + groups - offset, groups))
        return cache[offset]

    up, down = 0.0, 0.0
    for step in range(1, groups):
        up = lax.ppermute(at(step) + up, "filter", [(i, i + 1) for i in range(step)])
        down = lax.ppermute(
            at(groups - step) + down, "filter", [(i, i - 1) for i in range(groups - step, groups)]
        )
    return at(0) + up + down


def swap(value, bit, size):
    return lax.ppermute(value, "dp", [(i, i ^ (1 << bit)) for i in range(size)])


def pick(value, axis, index):
    return lax.dynamic_index_in_dim(value, index, axis, keepdims=False)


def by_permutes(inputs, kernel, cotangent):
    sample = inputs[0]
    height, width, local_in = sample.shape
    channels = kernel.shape[3]
    groups = lax.axis_size("filter")
    samples = lax.axis_size("dp")
    position = lax.axis_index("filter")
    place = lax.axis_index("dp")
    bits = samples.bit_length() - 1
    mine = [(place >> bit) & 1 for bit in range(bits)]
    my_rows = height // groups
    pad = ((1, 1), (1, 1), (0, 0))

    other = swap(sample, 0, samples)
    grad_rows = gather_rows(cotangent[0], groups, position)

    xpad = jnp.pad(sample, pad)

    def partial(block):
        rows = lax.dynamic_slice_in_dim(xpad, block * my_rows, my_rows + 2, 0)
        return lax.conv_general_dilated(
            rows[None], kernel, (1, 1), "VALID",
            dimension_numbers=("NHWC", "HWIO", "NHWC"),
            preferred_element_type=jnp.float32,
        )[0]

    outputs = scatter_rows(partial, groups, position).astype(jnp.bfloat16)[None]

    split = grad_rows.reshape(height, width, samples // 2, 2, channels // samples)
    own_half = pick(split, 3, mine[0])
    other_half = swap(pick(split, 3, 1 - mine[0]), 0, samples)
    pair_x = jnp.stack([xpad, jnp.pad(other, pad)])
    pair_g = jnp.stack([own_half, other_half])
    part = channels // samples // 2
    rest = list(range(1, bits))

    def weight_grad(cols):
        taps = [
            jnp.einsum(
                "nhwi,nhwo->oi",
                pair_x[:, a : a + height, b : b + width],
                cols,
                preferred_element_type=jnp.float32,
            )
            for a in range(3)
            for b in range(3)
        ]
        return jnp.stack(taps)

    plans = [rest, rest[::-1]]

    def columns(number, which):
        order = plans[number]
        cols = pair_g[..., number * part : (number + 1) * part]
        cols = cols.reshape((2, height, width) + (2,) * len(rest) + (part,))
        axis = 3 + (bits - 1 - order[0])
        index = mine[order[0]]
        chosen = pick(cols, axis, index if which else 1 - index)
        return chosen.reshape(2, height, width, -1)

    sent = weight_grad(jnp.concatenate([columns(0, False), columns(1, False)], -1))
    kept = weight_grad(jnp.concatenate([columns(0, True), columns(1, True)], -1))
    half = sent.shape[1] // 2
    finals = []
    for number, order in enumerate(plans):
        send = sent[:, number * half : (number + 1) * half]
        keep = kept[:, number * half : (number + 1) * half]
        left = sorted(order, reverse=True)
        for stage, bit in enumerate(order):
            total = keep + swap(send, bit, samples)
            left.remove(bit)
            if stage + 1 < len(order):
                total = total.reshape((9,) + (2,) * len(left) + (part, local_in))
                following = order[stage + 1]
                axis = 1 + left.index(following)
                send = pick(total, axis, 1 - mine[following]).reshape(9, -1, local_in)
                keep = pick(total, axis, mine[following]).reshape(9, -1, local_in)
        finals.append(total)
    scale = 1.0 / jnp.sqrt(jnp.float32(samples * height * width))
    grads = jnp.concatenate(finals, 1) * scale
    kernel_grad = grads.transpose(1, 0, 2).reshape(-1, 3, 3, local_in)

    input_grad = lax.conv_general_dilated(
        grad_rows[None], kernel[::-1, ::-1], (1, 1), "SAME",
        dimension_numbers=("NHWC", "HWOI", "NHWC"),
        preferred_element_type=jnp.float32,
    ).astype(jnp.bfloat16)
    return (outputs, input_grad, kernel_grad)


F32, BF16 = jnp.float32, jnp.bfloat16


def spread(x_ref, wide_ref, tall_ref, width):
    cells, lanes = x_ref.shape
    values = x_ref[...].astype(F32)
    column = lax.rem(lax.broadcasted_iota(jnp.int32, (cells, lanes), 0), width)
    edge = jnp.zeros((width, lanes), F32)
    tall_ref[:width] = edge
    tall_ref[width + cells :] = edge
    for b in range(3):
        if b == 0:
            moved = jnp.where(column == 0, 0.0, pltpu.roll(values, 1, 0))
        elif b == 1:
            moved = values
        else:
            moved = jnp.where(column == width - 1, 0.0, pltpu.roll(values, cells - 1, 0))
        tall_ref[width : width + cells] = moved
        for a in range(3):
            tap = 3 * a + b
            wide_ref[:, tap * lanes : (tap + 1) * lanes] = tall_ref[
                a * width : a * width + cells
            ].astype(BF16)


def step_kernel(
    n, width, scale, x_ref, k_ref, g_ref,
    out_ref, dx_ref, dk_ref,
    x_other, wide, wide_other, tall, tall_sum, g_all, g_other, g_turned,
    parts, own, from_below, from_above, weights, first_a, first_b, second,
    x_sem, gather_send, gather_recv, pair_send, pair_recv, up_send, up_recv,
    down_send, down_recv, one_send, one_recv, two_send, two_recv,
):
    cells, lanes = x_ref.shape
    rows, channels = g_ref.shape
    z = lax.axis_index("filter")
    d = lax.axis_index("dp")
    core, x, y = lax.rem(d, 2), lax.rem(d // 2, 2), d // 4
    partner, along_x, along_y = d + 1 - 2 * core, d + 2 - 4 * x, d + 4 - 8 * y
    block = dk_ref.shape[1]
    half = block // 2

    def remote(source, target, send, recv, **where):
        return pltpu.make_async_remote_copy(
            src_ref=source, dst_ref=target, send_sem=send, recv_sem=recv,
            device_id=where, device_id_type=pl.DeviceIdType.MESH,
        )

    def at_rows(index):
        return pl.ds(pl.multiple_of(index * rows, rows), rows)

    barrier = pltpu.get_barrier_semaphore()
    for offset in range(1, n):
        pl.semaphore_signal(barrier, inc=1, device_id={"filter": lax.rem(z + offset, n)},
                            device_id_type=pl.DeviceIdType.MESH)
    for peer in (partner, along_x, along_y):
        pl.semaphore_signal(barrier, inc=1, device_id={"dp": peer},
                            device_id_type=pl.DeviceIdType.MESH)
    pl.semaphore_wait(barrier, n + 2)

    def gather(offset):
        return remote(g_ref, g_all.at[at_rows(z)], gather_send.at[offset], gather_recv.at[z],
                      filter=lax.rem(z + offset, n))

    order = [n // 2] + [s for s in range(1, n) if s != n // 2]
    for offset in order:
        gather(offset).start()
    share = remote(x_ref, x_other, x_sem.at[0], x_sem.at[1], dp=partner)
    share.start()

    def pair_copy(source, offset, q, j):
        columns = pl.ds(pl.multiple_of((2 * j + 1 - core) * block, block), block)
        rows_from = source.at[:, columns] if offset == 0 else source.at[at_rows(q), columns]
        return remote(rows_from, g_other.at[at_rows(q), pl.ds(j * block, block)],
                      pair_send.at[offset, j], pair_recv.at[offset, j], dp=partner)

    for j in range(4):
        pair_copy(g_ref, 0, z, j).start()
    g_all[at_rows(z), :] = g_ref[...]

    spread(x_ref, wide, tall, width)

    def send_up(s):
        return remote(parts.at[s], from_below.at[s], up_send.at[s], up_recv.at[s], filter=z + 1)

    def send_down(s):
        return remote(parts.at[n - s], from_above.at[s], down_send.at[s], down_recv.at[s],
                      filter=z - 1)

    def partial(offset, store):
        source = at_rows(lax.rem(z + n - offset, n))

        @pl.loop(0, channels // 256)
        def _(part):
            columns = pl.ds(pl.multiple_of(part * 256, 256), 256)
            store(columns, jnp.dot(wide[source, :], k_ref[:, columns], preferred_element_type=F32))

    @pl.loop(1, n)
    def _(k):
        offset = jnp.where(2 * z < n, k, n - k)

        def store(columns, value):
            parts[offset, :, columns] = value

        partial(offset, store)

        @pl.when(z == 0)
        def _():
            send_up(k).start()

        @pl.when(z == n - 1)
        def _():
            send_down(k).start()

    def store_own(columns, value):
        own[:, columns] = value

    partial(0, store_own)
    share.wait()
    spread(x_other, wide_other, tall, width)

    def relay(s):
        @pl.when((z >= 1) & (z < s) & (z < n - 1))
        def _():
            send_up(s - 1).wait_recv()
            parts[s] += from_below[s - 1]
            send_up(s).start()

        @pl.when((z <= n - 2) & (n - 1 - z < s) & (z > 0))
        def _():
            send_down(s - 1).wait_recv()
            parts[n - s] += from_above[s - 1]
            send_down(s).start()

    arrivals = [s for s in range(1, n)]
    for offset in arrivals:
        q = lax.rem(z + offset, n)
        remote(g_ref, g_all.at[at_rows(q)], gather_send.at[offset], gather_recv.at[q],
               filter=q).wait_recv()
        for j in range(4):
            pair_copy(g_all, offset, q, j).start()
    relay(2)
    for offset in range(n):
        q = lax.rem(z + offset, n)
        for j in range(4):
            pair_copy(g_ref if offset == 0 else g_all, offset, q, j).wait()

    def weight_block(j):
        columns = pl.ds(pl.multiple_of((2 * j + core) * block, block), block)
        g_turned[:, :cells] = g_all[:, columns].T
        g_turned[:, cells:] = g_other[:, pl.ds(pl.multiple_of(j * block, block), block)].T

        @pl.loop(0, 9)
        def _(tap):
            taps = pl.ds(pl.multiple_of(tap * lanes, lanes), lanes)
            weights[j, tap] = jnp.dot(
                g_turned[:, :cells], wide[:, taps], preferred_element_type=F32
            ) + jnp.dot(g_turned[:, cells:], wide_other[:, taps], preferred_element_type=F32)

    low, high = pl.ds(0, half), pl.ds(half, half)

    def first_x(iy):
        return remote(weights.at[2 * iy + 1 - x, :, low], first_a.at[iy],
                      one_send.at[0, iy], one_recv.at[0, iy], dp=along_x)

    def first_y(ix):
        return remote(weights.at[2 * (1 - y) + ix, :, high], first_b.at[ix],
                      one_send.at[1, ix], one_recv.at[1, ix], dp=along_y)

    @pl.loop(0, 4)
    def _(turn):
        flip_y = 1 - lax.rem(turn, 2)
        flip_x = 1 - turn // 2
        iy = y + flip_y - 2 * y * flip_y
        ix = x + flip_x - 2 * x * flip_x
        weight_block(2 * iy + ix)

        @pl.when(flip_x == 1)
        def _():
            first_x(iy).start()

        @pl.when(flip_y == 1)
        def _():
            first_y(ix).start()

    column = lax.rem(lax.broadcasted_iota(jnp.int32, (cells, lanes), 0), width)
    for b in (1, 0, 2):
        tall[...] = jnp.zeros(tall.shape, F32)
        for a in range(3):
            tap = 3 * a + b

            @pl.loop(0, n)
            def _(q, tap=tap, a=a):
                place = pl.ds(pl.multiple_of(q * rows + a * width, 8), rows)
                tall[place, :] += lax.dot_general(
                    g_all[at_rows(q), :], k_ref[tap * lanes : (tap + 1) * lanes, :],
                    (((1,), (1,)), ((), ())), preferred_element_type=F32,
                )

        found = tall[width : width + cells]
        if b == 1:
            tall_sum[...] = found
        elif b == 0:
            tall_sum[...] += jnp.where(column == width - 1, 0.0, pltpu.roll(found, cells - 1, 0))
        else:
            tall_sum[...] += jnp.where(column == 0, 0.0, pltpu.roll(found, 1, 0))
    dx_ref[...] = tall_sum[...].astype(BF16)

    relay(3)

    first_x(1 - y).wait_recv()
    weights[2 * (1 - y) + x, :, low] += first_a[1 - y]
    last_y = remote(weights.at[2 * (1 - y) + x, :, low], second.at[0], two_send.at[0],
                    two_recv.at[0], dp=along_y)
    last_y.start()
    first_y(1 - x).wait_recv()
    weights[2 * y + 1 - x, :, high] += first_b[1 - x]
    last_x = remote(weights.at[2 * y + 1 - x, :, high], second.at[1], two_send.at[1],
                    two_recv.at[1], dp=along_x)
    last_x.start()
    first_x(y).wait_recv()
    first_y(x).wait_recv()
    for s in range(4, n):
        relay(s)
    last_y.wait()
    last_x.wait()
    mine = 2 * y + x
    dk_ref[:, :half] = (weights[mine, :, :half] + first_a[y] + second[0]) * scale
    dk_ref[:, half:] = (weights[mine, :, half:] + first_b[x] + second[1]) * scale

    @pl.when(z >= 1)
    def _():
        send_up(n - 1).wait_recv()
        own[...] += from_below[n - 1]

    @pl.when(z <= n - 2)
    def _():
        send_down(n - 1).wait_recv()
        own[...] += from_above[n - 1]

    out_ref[...] = own[...].astype(BF16)

    for offset in range(1, n):
        gather(offset).wait_send()
    for index in range(2):
        first_x(index).wait_send()
        first_y(index).wait_send()
    for s in range(1, n):
        @pl.when((z < s) & (z < n - 1))
        def _(s=s):
            send_up(s).wait_send()

        @pl.when((n - 1 - z < s) & (z > 0))
        def _(s=s):
            send_down(s).wait_send()


def on_device(inputs, kernel, cotangent):
    _, height, width, lanes = inputs.shape
    channels = kernel.shape[3]
    n = lax.axis_size("filter")
    samples = lax.axis_size("dp")
    rows, cells, block = height // n * width, height * width, channels // samples
    if samples != 8 or n != 4 or block % 128 or rows % 32 or lanes % 128 or channels % 256:
        return by_permutes(inputs, kernel, cotangent)
    scale = (samples * cells) ** -0.5
    vmem = pl.BlockSpec(memory_space=pltpu.VMEM)
    dma = pltpu.SemaphoreType.DMA
    outputs, input_grad, grads = pl.pallas_call(
        functools.partial(step_kernel, n, width, scale),
        out_shape=(
            jax.ShapeDtypeStruct((rows, channels), BF16),
            jax.ShapeDtypeStruct((cells, lanes), BF16),
            jax.ShapeDtypeStruct((9, block, lanes), F32),
        ),
        in_specs=[vmem] * 3,
        out_specs=(vmem,) * 3,
        scratch_shapes=[
            pltpu.VMEM((cells, lanes), BF16),
            pltpu.VMEM((cells, 9 * lanes), BF16),
            pltpu.VMEM((cells, 9 * lanes), BF16),
            pltpu.VMEM((cells + 2 * width, lanes), F32),
            pltpu.VMEM((cells, lanes), F32),
            pltpu.VMEM((cells, channels), BF16),
            pltpu.VMEM((cells, channels // 2), BF16),
            pltpu.VMEM((block, 2 * cells), BF16),
            pltpu.VMEM((n, rows, channels), F32),
            pltpu.VMEM((rows, channels), F32),
            pltpu.VMEM((n, rows, channels), F32),
            pltpu.VMEM((n, rows, channels), F32),
            pltpu.VMEM((4, 9, block, lanes), F32),
            pltpu.VMEM((2, 9, block // 2, lanes), F32),
            pltpu.VMEM((2, 9, block // 2, lanes), F32),
            pltpu.VMEM((2, 9, block // 2, lanes), F32),
            dma((2,)), dma((n,)), dma((n,)), dma((n, 4)), dma((n, 4)),
            dma((n,)), dma((n,)), dma((n,)), dma((n,)),
            dma((2, 2)), dma((2, 2)), dma((2,)), dma((2,)),
        ],
        compiler_params=pltpu.CompilerParams(
            collective_id=0, has_side_effects=True, vmem_limit_bytes=62 * 2**20
        ),
    )(
        inputs.reshape(cells, lanes),
        kernel.reshape(9 * lanes, channels),
        cotangent.reshape(rows, channels),
    )
    return (
        outputs.reshape(1, height // n, width, channels),
        input_grad.reshape(1, height, width, lanes),
        grads.transpose(1, 0, 2).reshape(block, 3, 3, lanes),
    )


def solution(mesh):
    return jax.shard_map(
        on_device,
        mesh=mesh,
        in_specs=(
            P("dp", None, None, "filter"),
            P(None, None, "filter", None),
            P("dp", "filter", None, None),
        ),
        out_specs=(
            P("dp", "filter", None, None),
            P("dp", None, None, "filter"),
            P("dp", None, None, "filter"),
        ),
        check_vma=False,
    )
```

```python
import functools

import jax
import jax.numpy as jnp
from jax import lax
from jax.experimental import pallas as pl
from jax.experimental.pallas import tpu as pltpu
from jax.sharding import PartitionSpec as P


def gather_rows(block, groups, position):
    up, down = block, block
    above, below = [], []
    for step in range(1, groups):
        up = lax.ppermute(up, "filter", [(i, i + 1) for i in range(step - 1, groups - 1)])
        down = lax.ppermute(down, "filter", [(i, i - 1) for i in range(1, groups - step + 1)])
        below.insert(0, up)
        above.append(down)
    rows = block.shape[0]
    line = jnp.concatenate(below + [block] + above, 0)
    return lax.dynamic_slice_in_dim(line, (groups - 1 - position) * rows, groups * rows, 0)


def scatter_rows(partial, groups, position):
    cache = {}

    def at(offset):
        offset = offset % groups
        if offset not in cache:
            cache[offset] = partial(lax.rem(position + groups - offset, groups))
        return cache[offset]

    up, down = 0.0, 0.0
    for step in range(1, groups):
        up = lax.ppermute(at(step) + up, "filter", [(i, i + 1) for i in range(step)])
        down = lax.ppermute(
            at(groups - step) + down, "filter", [(i, i - 1) for i in range(groups - step, groups)]
        )
    return at(0) + up + down


def swap(value, bit, size):
    return lax.ppermute(value, "dp", [(i, i ^ (1 << bit)) for i in range(size)])


def pick(value, axis, index):
    return lax.dynamic_index_in_dim(value, index, axis, keepdims=False)


def by_permutes(inputs, kernel, cotangent):
    sample = inputs[0]
    height, width, local_in = sample.shape
    channels = kernel.shape[3]
    groups = lax.axis_size("filter")
    samples = lax.axis_size("dp")
    position = lax.axis_index("filter")
    place = lax.axis_index("dp")
    bits = samples.bit_length() - 1
    mine = [(place >> bit) & 1 for bit in range(bits)]
    my_rows = height // groups
    pad = ((1, 1), (1, 1), (0, 0))

    other = swap(sample, 0, samples)
    grad_rows = gather_rows(cotangent[0], groups, position)

    xpad = jnp.pad(sample, pad)

    def partial(block):
        rows = lax.dynamic_slice_in_dim(xpad, block * my_rows, my_rows + 2, 0)
        return lax.conv_general_dilated(
            rows[None], kernel, (1, 1), "VALID",
            dimension_numbers=("NHWC", "HWIO", "NHWC"),
            preferred_element_type=jnp.float32,
        )[0]

    outputs = scatter_rows(partial, groups, position).astype(jnp.bfloat16)[None]

    split = grad_rows.reshape(height, width, samples // 2, 2, channels // samples)
    own_half = pick(split, 3, mine[0])
    other_half = swap(pick(split, 3, 1 - mine[0]), 0, samples)
    pair_x = jnp.stack([xpad, jnp.pad(other, pad)])
    pair_g = jnp.stack([own_half, other_half])
    part = channels // samples // 2
    rest = list(range(1, bits))

    def weight_grad(cols):
        taps = [
            jnp.einsum(
                "nhwi,nhwo->oi",
                pair_x[:, a : a + height, b : b + width],
                cols,
                preferred_element_type=jnp.float32,
            )
            for a in range(3)
            for b in range(3)
        ]
        return jnp.stack(taps)

    plans = [rest, rest[::-1]]

    def columns(number, which):
        order = plans[number]
        cols = pair_g[..., number * part : (number + 1) * part]
        cols = cols.reshape((2, height, width) + (2,) * len(rest) + (part,))
        axis = 3 + (bits - 1 - order[0])
        index = mine[order[0]]
        chosen = pick(cols, axis, index if which else 1 - index)
        return chosen.reshape(2, height, width, -1)

    sent = weight_grad(jnp.concatenate([columns(0, False), columns(1, False)], -1))
    kept = weight_grad(jnp.concatenate([columns(0, True), columns(1, True)], -1))
    half = sent.shape[1] // 2
    finals = []
    for number, order in enumerate(plans):
        send = sent[:, number * half : (number + 1) * half]
        keep = kept[:, number * half : (number + 1) * half]
        left = sorted(order, reverse=True)
        for stage, bit in enumerate(order):
            total = keep + swap(send, bit, samples)
            left.remove(bit)
            if stage + 1 < len(order):
                total = total.reshape((9,) + (2,) * len(left) + (part, local_in))
                following = order[stage + 1]
                axis = 1 + left.index(following)
                send = pick(total, axis, 1 - mine[following]).reshape(9, -1, local_in)
                keep = pick(total, axis, mine[following]).reshape(9, -1, local_in)
        finals.append(total)
    scale = 1.0 / jnp.sqrt(jnp.float32(samples * height * width))
    grads = jnp.concatenate(finals, 1) * scale
    kernel_grad = grads.transpose(1, 0, 2).reshape(-1, 3, 3, local_in)

    input_grad = lax.conv_general_dilated(
        grad_rows[None], kernel[::-1, ::-1], (1, 1), "SAME",
        dimension_numbers=("NHWC", "HWOI", "NHWC"),
        preferred_element_type=jnp.float32,
    ).astype(jnp.bfloat16)
    return (outputs, input_grad, kernel_grad)


F32, BF16 = jnp.float32, jnp.bfloat16


def spread(x_ref, wide_ref, tall_ref, width):
    cells, lanes = x_ref.shape
    values = x_ref[...].astype(F32)
    column = lax.rem(lax.broadcasted_iota(jnp.int32, (cells, lanes), 0), width)
    edge = jnp.zeros((width, lanes), F32)
    tall_ref[:width] = edge
    tall_ref[width + cells :] = edge
    for b in range(3):
        if b == 0:
            moved = jnp.where(column == 0, 0.0, pltpu.roll(values, 1, 0))
        elif b == 1:
            moved = values
        else:
            moved = jnp.where(column == width - 1, 0.0, pltpu.roll(values, cells - 1, 0))
        tall_ref[width : width + cells] = moved
        for a in range(3):
            tap = 3 * a + b
            wide_ref[:, tap * lanes : (tap + 1) * lanes] = tall_ref[
                a * width : a * width + cells
            ].astype(BF16)


def step_kernel(
    n, width, scale, x_ref, k_ref, g_ref,
    out_ref, dx_ref, dk_ref,
    x_other, wide, wide_other, tall, tall_sum, g_all, g_other, g_turned,
    parts, own, from_below, from_above, weights, first_a, first_b, second,
    x_sem, gather_send, gather_recv, pair_send, pair_recv, up_send, up_recv,
    down_send, down_recv, one_send, one_recv, two_send, two_recv,
):
    cells, lanes = x_ref.shape
    rows, channels = g_ref.shape
    z = lax.axis_index("filter")
    d = lax.axis_index("dp")
    core, x, y = lax.rem(d, 2), lax.rem(d // 2, 2), d // 4
    partner, along_x, along_y = d + 1 - 2 * core, d + 2 - 4 * x, d + 4 - 8 * y
    block = dk_ref.shape[1]
    half = block // 2

    def remote(source, target, send, recv, **where):
        return pltpu.make_async_remote_copy(
            src_ref=source, dst_ref=target, send_sem=send, recv_sem=recv,
            device_id=where, device_id_type=pl.DeviceIdType.MESH,
        )

    def at_rows(index):
        return pl.ds(pl.multiple_of(index * rows, rows), rows)

    barrier = pltpu.get_barrier_semaphore()
    for offset in range(1, n):
        pl.semaphore_signal(barrier, inc=1, device_id={"filter": lax.rem(z + offset, n)},
                            device_id_type=pl.DeviceIdType.MESH)
    for peer in (partner, along_x, along_y):
        pl.semaphore_signal(barrier, inc=1, device_id={"dp": peer},
                            device_id_type=pl.DeviceIdType.MESH)
    pl.semaphore_wait(barrier, n + 2)

    def pass_up(step):
        source = g_ref if step == 0 else g_all.at[at_rows(z - step)]
        return remote(source, g_all.at[at_rows(z - step)], gather_send.at[0, step],
                      gather_recv.at[z - step], filter=z + 1)

    def pass_down(step):
        source = g_ref if step == 0 else g_all.at[at_rows(z + step)]
        return remote(source, g_all.at[at_rows(z + step)], gather_send.at[1, step],
                      gather_recv.at[z + step], filter=z - 1)

    @pl.when(z < n - 1)
    def _():
        pass_up(0).start()

    @pl.when(z > 0)
    def _():
        pass_down(0).start()

    share = remote(x_ref, x_other, x_sem.at[0], x_sem.at[1], dp=partner)
    share.start()

    def pair_copy(source, q, j):
        columns = pl.ds(pl.multiple_of((2 * j + 1 - core) * block, block), block)
        rows_from = source.at[:, columns] if source is g_ref else source.at[at_rows(q), columns]
        return remote(rows_from, g_other.at[at_rows(q), pl.ds(j * block, block)],
                      pair_send.at[q, j], pair_recv.at[q, j], dp=partner)

    for j in range(4):
        pair_copy(g_ref, z, j).start()
    g_all[at_rows(z), :] = g_ref[...]

    spread(x_ref, wide, tall, width)

    def send_up(s):
        return remote(parts.at[s], from_below.at[s], up_send.at[s], up_recv.at[s], filter=z + 1)

    def send_down(s):
        return remote(parts.at[n - s], from_above.at[s], down_send.at[s], down_recv.at[s],
                      filter=z - 1)

    def partial(offset, store):
        source = at_rows(lax.rem(z + n - offset, n))

        @pl.loop(0, channels // 256)
        def _(part):
            columns = pl.ds(pl.multiple_of(part * 256, 256), 256)
            store(columns, jnp.dot(wide[source, :], k_ref[:, columns], preferred_element_type=F32))

    @pl.loop(1, n)
    def _(k):
        offset = jnp.where(2 * z < n, k, n - k)

        def store(columns, value):
            parts[offset, :, columns] = value

        partial(offset, store)

        @pl.when(z == 0)
        def _():
            send_up(k).start()

        @pl.when(z == n - 1)
        def _():
            send_down(k).start()

    def store_own(columns, value):
        own[:, columns] = value

    def arrive(step):
        @pl.when(z >= step)
        def _():
            q = z - step
            remote(g_ref, g_all.at[at_rows(q)], gather_send.at[0, step], gather_recv.at[q],
                   filter=q).wait_recv()

            @pl.when(z < n - 1)
            def _():
                pass_up(step).start()

            for j in range(4):
                pair_copy(g_all, q, j).start()

        @pl.when(z + step < n)
        def _():
            q = z + step
            remote(g_ref, g_all.at[at_rows(q)], gather_send.at[1, step], gather_recv.at[q],
                   filter=q).wait_recv()

            @pl.when(z > 0)
            def _():
                pass_down(step).start()

            for j in range(4):
                pair_copy(g_all, q, j).start()

    arrive(1)
    partial(0, store_own)
    share.wait()
    spread(x_other, wide_other, tall, width)
    for step in range(2, n):
        arrive(step)

    def relay(s):
        @pl.when((z >= 1) & (z < s) & (z < n - 1))
        def _():
            send_up(s - 1).wait_recv()
            parts[s] += from_below[s - 1]
            send_up(s).start()

        @pl.when((z <= n - 2) & (n - 1 - z < s) & (z > 0))
        def _():
            send_down(s - 1).wait_recv()
            parts[n - s] += from_above[s - 1]
            send_down(s).start()

    relay(2)
    for q in range(n):
        for j in range(4):
            pair_copy(g_all, q, j).wait()

    def weight_block(j):
        columns = pl.ds(pl.multiple_of((2 * j + core) * block, block), block)
        g_turned[:, :cells] = g_all[:, columns].T
        g_turned[:, cells:] = g_other[:, pl.ds(pl.multiple_of(j * block, block), block)].T

        @pl.loop(0, 9)
        def _(tap):
            taps = pl.ds(pl.multiple_of(tap * lanes, lanes), lanes)
            weights[j, tap] = jnp.dot(
                g_turned[:, :cells], wide[:, taps], preferred_element_type=F32
            ) + jnp.dot(g_turned[:, cells:], wide_other[:, taps], preferred_element_type=F32)

    low, high = pl.ds(0, half), pl.ds(half, half)

    def first_x(iy):
        return remote(weights.at[2 * iy + 1 - x, :, low], first_a.at[iy],
                      one_send.at[0, iy], one_recv.at[0, iy], dp=along_x)

    def first_y(ix):
        return remote(weights.at[2 * (1 - y) + ix, :, high], first_b.at[ix],
                      one_send.at[1, ix], one_recv.at[1, ix], dp=along_y)

    @pl.loop(0, 4)
    def _(turn):
        flip_y = 1 - lax.rem(turn, 2)
        flip_x = 1 - turn // 2
        iy = y + flip_y - 2 * y * flip_y
        ix = x + flip_x - 2 * x * flip_x
        weight_block(2 * iy + ix)

        @pl.when(flip_x == 1)
        def _():
            first_x(iy).start()

        @pl.when(flip_y == 1)
        def _():
            first_y(ix).start()

    column = lax.rem(lax.broadcasted_iota(jnp.int32, (cells, lanes), 0), width)
    for b in (1, 0, 2):
        tall[...] = jnp.zeros(tall.shape, F32)
        for a in range(3):
            tap = 3 * a + b

            @pl.loop(0, n)
            def _(q, tap=tap, a=a):
                place = pl.ds(pl.multiple_of(q * rows + a * width, 8), rows)
                tall[place, :] += lax.dot_general(
                    g_all[at_rows(q), :], k_ref[tap * lanes : (tap + 1) * lanes, :],
                    (((1,), (1,)), ((), ())), preferred_element_type=F32,
                )

        found = tall[width : width + cells]
        if b == 1:
            tall_sum[...] = found
        elif b == 0:
            tall_sum[...] += jnp.where(column == width - 1, 0.0, pltpu.roll(found, cells - 1, 0))
        else:
            tall_sum[...] += jnp.where(column == 0, 0.0, pltpu.roll(found, 1, 0))
    dx_ref[...] = tall_sum[...].astype(BF16)

    relay(3)

    first_x(1 - y).wait_recv()
    weights[2 * (1 - y) + x, :, low] += first_a[1 - y]
    last_y = remote(weights.at[2 * (1 - y) + x, :, low], second.at[0], two_send.at[0],
                    two_recv.at[0], dp=along_y)
    last_y.start()
    first_y(1 - x).wait_recv()
    weights[2 * y + 1 - x, :, high] += first_b[1 - x]
    last_x = remote(weights.at[2 * y + 1 - x, :, high], second.at[1], two_send.at[1],
                    two_recv.at[1], dp=along_x)
    last_x.start()
    first_x(y).wait_recv()
    first_y(x).wait_recv()
    for s in range(4, n):
        relay(s)
    last_y.wait()
    last_x.wait()
    mine = 2 * y + x
    dk_ref[:, :half] = (weights[mine, :, :half] + first_a[y] + second[0]) * scale
    dk_ref[:, half:] = (weights[mine, :, half:] + first_b[x] + second[1]) * scale

    @pl.when(z >= 1)
    def _():
        send_up(n - 1).wait_recv()
        own[...] += from_below[n - 1]

    @pl.when(z <= n - 2)
    def _():
        send_down(n - 1).wait_recv()
        own[...] += from_above[n - 1]

    out_ref[...] = own[...].astype(BF16)

    for step in range(n - 1):
        @pl.when((z >= step) & (z < n - 1))
        def _(step=step):
            pass_up(step).wait_send()

        @pl.when((z + step < n) & (z > 0))
        def _(step=step):
            pass_down(step).wait_send()

    for index in range(2):
        first_x(index).wait_send()
        first_y(index).wait_send()
    for s in range(1, n):
        @pl.when((z < s) & (z < n - 1))
        def _(s=s):
            send_up(s).wait_send()

        @pl.when((n - 1 - z < s) & (z > 0))
        def _(s=s):
            send_down(s).wait_send()


def on_device(inputs, kernel, cotangent):
    _, height, width, lanes = inputs.shape
    channels = kernel.shape[3]
    n = lax.axis_size("filter")
    samples = lax.axis_size("dp")
    rows, cells, block = height // n * width, height * width, channels // samples
    if samples != 8 or n != 4 or block % 128 or rows % 32 or lanes % 128 or channels % 256:
        return by_permutes(inputs, kernel, cotangent)
    scale = (samples * cells) ** -0.5
    vmem = pl.BlockSpec(memory_space=pltpu.VMEM)
    dma = pltpu.SemaphoreType.DMA
    outputs, input_grad, grads = pl.pallas_call(
        functools.partial(step_kernel, n, width, scale),
        out_shape=(
            jax.ShapeDtypeStruct((rows, channels), BF16),
            jax.ShapeDtypeStruct((cells, lanes), BF16),
            jax.ShapeDtypeStruct((9, block, lanes), F32),
        ),
        in_specs=[vmem] * 3,
        out_specs=(vmem,) * 3,
        scratch_shapes=[
            pltpu.VMEM((cells, lanes), BF16),
            pltpu.VMEM((cells, 9 * lanes), BF16),
            pltpu.VMEM((cells, 9 * lanes), BF16),
            pltpu.VMEM((cells + 2 * width, lanes), F32),
            pltpu.VMEM((cells, lanes), F32),
            pltpu.VMEM((cells, channels), BF16),
            pltpu.VMEM((cells, channels // 2), BF16),
            pltpu.VMEM((block, 2 * cells), BF16),
            pltpu.VMEM((n, rows, channels), F32),
            pltpu.VMEM((rows, channels), F32),
            pltpu.VMEM((n, rows, channels), F32),
            pltpu.VMEM((n, rows, channels), F32),
            pltpu.VMEM((4, 9, block, lanes), F32),
            pltpu.VMEM((2, 9, block // 2, lanes), F32),
            pltpu.VMEM((2, 9, block // 2, lanes), F32),
            pltpu.VMEM((2, 9, block // 2, lanes), F32),
            dma((2,)), dma((2, n)), dma((n,)), dma((n, 4)), dma((n, 4)),
            dma((n,)), dma((n,)), dma((n,)), dma((n,)),
            dma((2, 2)), dma((2, 2)), dma((2,)), dma((2,)),
        ],
        compiler_params=pltpu.CompilerParams(
            collective_id=0, has_side_effects=True, vmem_limit_bytes=62 * 2**20
        ),
    )(
        inputs.reshape(cells, lanes),
        kernel.reshape(9 * lanes, channels),
        cotangent.reshape(rows, channels),
    )
    return (
        outputs.reshape(1, height // n, width, channels),
        input_grad.reshape(1, height, width, lanes),
        grads.transpose(1, 0, 2).reshape(block, 3, 3, lanes),
    )


def solution(mesh):
    return jax.shard_map(
        on_device,
        mesh=mesh,
        in_specs=(
            P("dp", None, None, "filter"),
            P(None, None, "filter", None),
            P("dp", "filter", None, None),
        ),
        out_specs=(
            P("dp", "filter", None, None),
            P("dp", None, None, "filter"),
            P("dp", None, None, "filter"),
        ),
        check_vma=False,
    )
```
